32 devices in a mesh: pos: 8 (over z, core), trk: 4 (over y, x).
Axes of the slice: x: 2, y: 2, z: 4, core: 2. Of those that a mesh axis runs over, the one named last changes fastest.
Arguments:
- activations: bfloat16 [4, 4096, 1536], P(None, 'pos', 'trk'), may hold values from -6 to 6
- norm_gain: float32 [1536], P('trk'), may hold values from 0.1 to 1.9
- norm_bias: float32 [1536], P('trk'), may hold values from -1 to 1
- conv_weight: bfloat16 [3, 1536, 1536], P(None, None, 'trk'), may hold values from -0.09375 to 0.09375
- head_weight: bfloat16 [1536, 4096], P(None, 'trk'), may hold values from -0.15625 to 0.15625
- head_bias: float32 [4096], P('trk'), may hold values from -2 to 0
- gene_slot: int32 [4, 4096], P(None, 'pos'), may hold values from -1 to 35, as said below
- straddle_map: int32 [32], P('pos'), may hold values from -1 to 31, as said below
Outputs:
- tracks: bfloat16 [4, 4096, 4096], P(None, 'pos', 'trk')
- gene_mean: float32 [256, 4096], P('pos', 'trk')
The draws below stay inside these ranges and needn't reach their ends.
Inputs may be any that keep to these rules, and one draw needn't show every extreme that they name: `gene_slot`: -1 marks a bin outside exons. A value g below 32 names gene g of the bin's own block of 512 positions; 32 + s names entry s of the previous block's straddle list and appears only where that entry is not -1, never in the first block. `straddle_map`: entry index * 4 + s names the gene of block index that entry s of its straddle list stands for, or -1; the live entries of one block are distinct, and the last block's are all -1.
All inputs are finite; a program needn't handle non-finite values.
Results may differ from the reference program's by a relative error of at most 0.0048.
Values may be sent and summed in bfloat16 or wider, within the bound.
No kernel may reach another device: no remote copies, remote signals or barrier semaphores. Data moves between devices by JAX's collectives and lax.ppermute only.
A program may use at most 128 MiB of HBM per device.

```python
import jax
import jax.numpy as jnp
from jax import lax

SEQS = 4
POS_DEV = 512
C = 1536
TRACKS = 4096
GENES_DEV = 32
STRAD = 4
LEN = 4096
GENES = 256
N_POS = 8


def gene_layout(key):
    base = jax.random.fold_in(key, 4099)
    key_flag, key_keep, key_exon = jax.random.split(base, 3)
    windows = GENES_DEV // SEQS
    span = POS_DEV // windows
    flags = jax.random.randint(key_flag, (N_POS, SEQS), 0, 2)
    not_last = (jnp.arange(N_POS) < N_POS - 1).astype(jnp.int32)
    flags = flags * not_last[:, None]
    keeping = jax.random.randint(key_keep, (N_POS, SEQS, windows), 0, 8) > 0
    exonic = jax.random.randint(key_exon, (N_POS, SEQS, POS_DEV), 0, 2) > 0
    offsets = jnp.arange(POS_DEV)
    window = offsets // span
    seq_ids = jnp.arange(SEQS)
    own_slot = seq_ids[None, :, None] * windows + window[None, None, :]
    forced = (window[None, None, :] == windows - 1) & (flags[:, :, None] > 0)
    alive = keeping[:, :, window] | forced
    previous = jnp.concatenate([jnp.zeros((1, SEQS), jnp.int32), flags[:-1]], axis=0)
    entering = (offsets[None, None, :] < span // 2) & (previous[:, :, None] > 0)
    slot_ids = jnp.where(entering, GENES_DEV + seq_ids[None, :, None], jnp.where(alive, own_slot, -1))
    slot_ids = jnp.where(exonic, slot_ids, -1)
    gene_slot = jnp.transpose(slot_ids, (1, 0, 2)).reshape(SEQS, N_POS * POS_DEV)
    straddle = jnp.where(flags > 0, seq_ids[None, :] * windows + windows - 1, -1).reshape(-1)
    return (gene_slot.astype(jnp.int32), straddle.astype(jnp.int32))


def draw_gene_slot(key, part):
    return gene_layout(key)[0]


def draw_straddle_map(key, part):
    return gene_layout(key)[1]


def levels(stream_key, extent, cuts, least, high):
    def one(axis_at, blocks):
        steps = jax.random.uniform(jax.random.fold_in(jax.random.fold_in(stream_key, 6), axis_at), (blocks,), jnp.float32, least / len(cuts), high / len(cuts))
        return jnp.repeat(jnp.exp(steps), extent[axis_at] // blocks).reshape((-1,) + (1,) * (len(extent) - axis_at - 1))

    level = one(*cuts[0])
    for cut in cuts[1:]:
        level = level * one(*cut)
    return level


def normal_values(key, extent, deviation, most, shards=(), held_as=jnp.bfloat16):
    level = levels(key, extent, shards, -0.22, 0.18) if shards else 1.0
    values = jax.random.normal(key, extent, jnp.float32) * deviation * level
    return jnp.minimum(jnp.maximum(values, -most), most).astype(held_as)


def setup_inputs(seed: int = 0) -> dict:
    splits = jax.random.split(jax.random.key(seed), 9)
    return {
        "activations": normal_values(splits[0], (SEQS, LEN, C), 1.0, 6.0, ((1, 8), (2, 4))),
        "norm_gain": jnp.clip(1.0 + 0.18 * jax.random.normal(splits[1], (C,), jnp.float32), 0.1, 1.9),
        "norm_bias": jnp.clip(jax.random.uniform(splits[2], (C,), jnp.float32, -1.0, 1.0) * levels(splits[2], (C,), ((0, 4),), -0.4, 0.0), -1.0, 1.0),
        "conv_weight": normal_values(splits[3], (3, C, C), (3 * C) ** -0.5, 0.09375, ((2, 4),)),
        "head_weight": normal_values(splits[4], (C, TRACKS), C ** -0.5, 0.15625, ((1, 4),)),
        "head_bias": jnp.clip(-2.0 + 2.0 * jax.random.uniform(splits[5], (TRACKS,), jnp.float32) ** levels(splits[5], (TRACKS,), ((0, 4),), -0.2, 0.2), -2.0, 0.0),
        "gene_slot": draw_gene_slot(jax.random.fold_in(splits[8], 71), 0),
        "straddle_map": draw_straddle_map(jax.random.fold_in(splits[8], 71), 0),
    }


def reference(activations, norm_gain, norm_bias, conv_weight, head_weight, head_bias, gene_slot, straddle_map):
    def one_sequence(values):
        hidden = jax.nn.gelu(values.astype(jnp.float32) * norm_gain + norm_bias, approximate=True).astype(jnp.bfloat16)
        padded = jnp.pad(hidden, ((1, 1), (0, 0)))
        conv_out = jnp.zeros((LEN, C), jnp.float32)
        for offset in range(3):
            conv_out = conv_out + jnp.dot(padded[offset:offset + LEN], conv_weight[offset], preferred_element_type=jnp.float32)
        mixed = (values.astype(jnp.float32) + conv_out).astype(jnp.bfloat16)
        logits = jnp.dot(mixed, head_weight, preferred_element_type=jnp.float32)
        return jax.nn.softplus(logits + head_bias).astype(jnp.bfloat16)

    tracks = lax.map(one_sequence, activations)
    positions = jnp.arange(LEN, dtype=jnp.int32)
    block = (positions // POS_DEV).astype(jnp.int32)
    block = jnp.broadcast_to(block[None, :], gene_slot.shape)
    own_gene = block * GENES_DEV + gene_slot
    owner = jnp.maximum(block - 1, 0)
    entry = (owner * STRAD + jnp.clip(gene_slot - GENES_DEV, 0, STRAD - 1)).astype(jnp.int32)
    other_gene = owner * GENES_DEV + straddle_map[entry]
    gene_ids = jnp.where(gene_slot < 0, GENES, jnp.where(gene_slot < GENES_DEV, own_gene, other_gene)).astype(jnp.int32)
    flat_ids = gene_ids.reshape(-1)
    flat_tracks = tracks.reshape(-1, TRACKS).astype(jnp.float32)
    gene_sum = jax.ops.segment_sum(flat_tracks, flat_ids, num_segments=GENES + 1)[:GENES]
    gene_count = jax.ops.segment_sum(jnp.ones(flat_ids.shape, jnp.float32), flat_ids, num_segments=GENES + 1)[:GENES]
    gene_mean = gene_sum / jnp.maximum(gene_count, 1.0)[:, None]
    return tracks, gene_mean
```

```python
import jax
import jax.numpy as jnp
from jax import lax
from jax.sharding import PartitionSpec as P

GENES_DEV = 32


def swap(value, bit):
    count = lax.axis_size("trk")
    return lax.ppermute(value, "trk", [(i, i ^ bit) for i in range(count)])


def spread(own):
    count = lax.axis_size("trk")
    half = own.shape[0] // 2
    blocks = {0: own}
    for j in range(1, count):
        low, high = j & -j, 1 << (j.bit_length() - 1)
        if low == high:
            blocks[j] = swap(own, j)
        else:
            blocks[j] = jnp.concatenate(
                [swap(blocks[j ^ high][:half], high), swap(blocks[j ^ low][half:], low)]
            )
    return [blocks[j] for j in range(count)]


def passed_along(value, axis, steps):
    count = lax.axis_size(axis)
    initial, last = (max(0, -steps), min(count, count - steps))
    return lax.ppermute(value, axis, [(source, source + steps) for source in range(initial, last)])


def per_device(
    activations, norm_gain, norm_bias, conv_weight, head_weight, head_bias, gene_slot, straddle_map
):
    sequences, length, channels = activations.shape
    count = lax.axis_size("trk")
    mine = lax.axis_index("trk")
    group = sequences // 2

    def hidden_of(values):
        return jax.nn.gelu(
            values.astype(jnp.float32) * norm_gain + norm_bias, approximate=True
        ).astype(jnp.bfloat16)

    taps = [
        lax.dynamic_slice_in_dim(conv_weight, (mine ^ j) * channels, channels, axis=1)
        for j in range(count)
    ]
    heads = [
        lax.dynamic_slice_in_dim(head_weight, (mine ^ j) * channels, channels, axis=0)
        for j in range(count)
    ]
    hidden = [hidden_of(activations[i * group : (i + 1) * group]) for i in range(2)]
    blocks = [spread(h) for h in hidden]
    edges = jnp.stack(
        [
            passed_along(jnp.concatenate([h[:, -1] for h in hidden]), "pos", 1),
            passed_along(jnp.concatenate([h[:, 0] for h in hidden]), "pos", -1),
        ]
    )
    edge_blocks = spread(edges)

    stride = straddle_map.shape[0]
    slots = jnp.arange(GENES_DEV + stride, dtype=jnp.int32)
    tracks, sums, counts = [], 0.0, 0.0
    for i in range(2):
        span = slice(i * group, (i + 1) * group)
        total = 0.0
        for j in range(count):
            block = blocks[i][j]
            edge = edge_blocks[j][:, span]
            padded = jnp.concatenate([edge[0][:, None], block, edge[1][:, None]], axis=1)
            for k in range(3):
                window = padded[:, k : k + length].reshape(group * length, channels)
                total = total + jnp.dot(window, taps[j][k], preferred_element_type=jnp.float32)
        own = activations[span].reshape(group * length, channels).astype(jnp.float32)
        mixed = (own + total).astype(jnp.bfloat16).reshape(group, length, channels)
        logits = 0.0
        for j, block in enumerate(spread(mixed)):
            logits = logits + jnp.dot(
                block.reshape(group * length, channels), heads[j], preferred_element_type=jnp.float32
            )
        part = jax.nn.softplus(logits + head_bias).astype(jnp.bfloat16)
        onehot = (gene_slot[span].reshape(-1)[None, :] == slots[:, None]).astype(jnp.bfloat16)
        sums = sums + jnp.dot(onehot, part, preferred_element_type=jnp.float32)
        counts = counts + jnp.sum(onehot.astype(jnp.float32), axis=1)
        tracks.append(part.reshape(group, length, -1))
    received, received_counts = passed_along((sums[GENES_DEV:], counts[GENES_DEV:]), "pos", -1)
    owners = (straddle_map[:, None] == jnp.arange(GENES_DEV, dtype=jnp.int32)[None, :]).astype(
        jnp.float32
    )
    totals = sums[:GENES_DEV] + jnp.dot(owners.T, received, precision=lax.Precision.HIGHEST)
    gene_counts = counts[:GENES_DEV] + jnp.dot(
        owners.T, received_counts, precision=lax.Precision.HIGHEST
    )
    gene_mean = totals / jnp.maximum(gene_counts, 1.0)[:, None]
    return (jnp.concatenate(tracks), gene_mean)


def solution(mesh):
    in_specs = (
        P(None, "pos", "trk"),
        P("trk"),
        P("trk"),
        P(None, None, "trk"),
        P(None, "trk"),
        P("trk"),
        P(None, "pos"),
        P("pos"),
    )
    out_specs = (P(None, "pos", "trk"), P("pos", "trk"))
    return jax.shard_map(
        per_device, mesh=mesh, in_specs=in_specs, out_specs=out_specs, check_vma=False
    )
```

```python
import functools

import jax
import jax.numpy as jnp
from jax import lax
from jax.experimental import pallas as pl
from jax.experimental.pallas import tpu as pltpu
from jax.sharding import PartitionSpec as P


GENES_DEV = 32
LANES = 128
LIMIT = 24 << 20
EDGE = 16
SIDE = 8
VMEM = pl.BlockSpec(memory_space=pltpu.VMEM)
ANY = pl.BlockSpec(memory_space=pl.ANY)
SMEM = pl.BlockSpec(memory_space=pltpu.SMEM)


def swap(value, bit):
    count = lax.axis_size("trk")
    return lax.ppermute(value, "trk", [(i, i ^ bit) for i in range(count)])


def split_bits(j):
    return j & -j, 1 << (j.bit_length() - 1)


def passed_along(value, axis, steps):
    count = lax.axis_size(axis)
    initial, last = (max(0, -steps), min(count, count - steps))
    return lax.ppermute(value, axis, [(source, source + steps) for source in range(initial, last)])


def spread(own, cut, rows):
    count = lax.axis_size("trk")
    wholes, parts = {0: own}, {}

    def piece(j, part):
        if j in wholes:
            return wholes[j][:cut] if part == 0 else wholes[j][cut:rows]
        return parts[j][part]

    places = [[(own, 0, cut), (own, cut, rows - cut)]]
    for j in range(1, count):
        low, high = split_bits(j)
        if low == high:
            wholes[j] = swap(own, j)
            places.append([(wholes[j], 0, cut), (wholes[j], cut, rows - cut)])
        else:
            parts[j] = (swap(piece(j ^ high, 0), high), swap(piece(j ^ low, 1), low))
            places.append([(parts[j][0], 0, cut), (parts[j][1], 0, rows - cut)])
    return places, wholes


def gelu_of(values, gain, bias):
    return jax.nn.gelu(values.astype(jnp.float32) * gain + bias, approximate=True)


def first_kernel(group, act_ref, all_ref, gain_ref, bias_ref, out_ref, tail_ref, head_ref, edges, sems):
    sequences, length, channels = all_ref.shape
    gain, bias = gain_ref[...][None], bias_ref[...][None]
    copies = []
    for s in range(sequences):
        for side, start in enumerate((length - EDGE, 0)):
            copies.append(
                pltpu.make_async_copy(
                    all_ref.at[s, pl.ds(start, EDGE)], edges.at[s, side], sems.at[s, side]
                )
            )
            copies[-1].start()
    for copy in copies:
        copy.wait()
    index = lax.broadcasted_iota(jnp.int32, (SIDE, channels), 0)
    tails = jnp.zeros((SIDE, channels), jnp.float32)
    heads = tails
    for s in range(sequences):
        tail = edges[s, 0].astype(jnp.float32)[EDGE - 1 :]
        head = edges[s, 1].astype(jnp.float32)[:1]
        tails = jnp.where(index == s, tail, tails)
        heads = jnp.where(index == s, head, heads)
    tail_ref[...] = gelu_of(tails, gain, bias).astype(jnp.bfloat16)
    head_ref[...] = gelu_of(heads, gain, bias).astype(jnp.bfloat16)
    for s in range(group):
        out_ref[s * length : (s + 1) * length, :] = gelu_of(act_ref[s], gain, bias).astype(jnp.bfloat16)


def second_kernel(act_ref, gain_ref, bias_ref, tail_ref, head_ref, out_ref):
    group, length, _ = act_ref.shape
    gain, bias = gain_ref[...][None], bias_ref[...][None]
    for s in range(group):
        out_ref[s * length : (s + 1) * length, :] = gelu_of(act_ref[s], gain, bias).astype(jnp.bfloat16)
    rows = group * length
    out_ref[rows : rows + EDGE, :] = jnp.concatenate(
        [tail_ref[...].astype(jnp.float32), head_ref[...].astype(jnp.float32)]
    ).astype(jnp.bfloat16)


def rows_of(plan, refs, start, size):
    out = []
    for places in plan:
        row, found = 0, []
        for which, first, extent in places:
            low, high = max(start, row), min(start + size, row + extent)
            if low < high:
                found.append(refs[which][first + low - row : first + high - row, :])
            row += extent
        out.append(found[0] if len(found) == 1 else jnp.concatenate(found))
    return jnp.concatenate(out, axis=1)


def conv_kernel(first, group, plan, edge_plan, n_blocks, t_ref, act_ref, w_ref, *refs):
    blocks, out_ref = refs[:n_blocks], refs[n_blocks]
    _, length, channels = act_ref.shape
    t = t_ref[0]
    count = len(plan)
    starts = [pl.multiple_of((t ^ j) * channels, channels) for j in range(count)]
    weight = jnp.concatenate(
        [jnp.concatenate([w_ref[k, pl.ds(start, channels), :] for start in starts]) for k in range(3)], axis=1
    )
    edge = jnp.concatenate([blocks[which][start : start + EDGE, :] for which, start in edge_plan], axis=1)
    row = lax.broadcasted_iota(jnp.int32, (length, channels), 0)
    for s in range(group):
        values = jnp.concatenate([rows_of(plan, blocks, s * length, length), edge])
        made = jnp.dot(values, weight, preferred_element_type=jnp.float32)
        before, at, after = (made[:, k * channels : (k + 1) * channels] for k in range(3))
        place = length + first + s
        left = jnp.where(row == 0, before[place : place + 1], pltpu.roll(before[:length], 1, 0))
        place += SIDE
        right = jnp.where(
            row == length - 1, after[place : place + 1], pltpu.roll(after[:length], length - 1, 0)
        )
        total = act_ref[s].astype(jnp.float32) + ((left + at[:length]) + right)
        out_ref[s * length : (s + 1) * length, :] = total.astype(jnp.bfloat16)


def head_kernel(first, group, length, plan, n_blocks, last, t_ref, w_ref, bias_ref, slot_ref, *refs):
    blocks = refs[:n_blocks]
    refs = refs[n_blocks:]
    if last:
        own_in, strad_in, _ = refs[:3]
        refs = refs[3:]
    tracks_ref, own_ref, strad_ref, made, out_sems = refs
    t = t_ref[0]
    count = len(plan)
    channels = w_ref.shape[0] // count
    starts = [pl.multiple_of((t ^ j) * channels, channels) for j in range(count)]
    weight = jnp.concatenate([w_ref[pl.ds(start, channels), :] for start in starts])
    n_own, n_strad = own_ref.shape[0], strad_ref.shape[0]
    index = lax.broadcasted_iota(jnp.int32, (n_own + n_strad, length), 0)
    if last:
        sums = jnp.concatenate([own_in[...], strad_in[...]])
    else:
        sums = jnp.zeros((n_own + n_strad, w_ref.shape[1]), jnp.float32)
    bias = bias_ref[...][None]
    outs = []
    for s in range(group):
        logits = jnp.dot(rows_of(plan, blocks, s * length, length), weight, preferred_element_type=jnp.float32)
        logits = logits + bias
        part = jnp.maximum(logits, 0.0) + jnp.log1p(jnp.exp(-jnp.abs(logits)))
        made[s] = part.astype(jnp.bfloat16)
        outs.append(pltpu.make_async_copy(made.at[s], tracks_ref.at[first + s], out_sems.at[s]))
        outs[-1].start()
        onehot = (index == slot_ref[first + s : first + s + 1, :]).astype(jnp.bfloat16)
        sums = sums + jnp.dot(onehot, made[s], preferred_element_type=jnp.float32)
    own_ref[...] = sums[:n_own]
    strad_ref[...] = sums[n_own:]
    for copy in outs:
        copy.wait()


def arrays_of(places):
    arrays, plan = [], []

    def index(array):
        for i, other in enumerate(arrays):
            if other is array:
                return i
        arrays.append(array)
        return len(arrays) - 1

    for block in places:
        plan.append([(index(array), start, size) for array, start, size in block])
    return arrays, plan, index


def cost(flops, nbytes, calls=0):
    return pl.CostEstimate(flops=int(flops), bytes_accessed=int(nbytes), transcendentals=int(calls))


def by_kernels(
    activations, norm_gain, norm_bias, conv_weight, head_weight, head_bias, gene_slot, straddle_map
):
    sequences, length, channels = activations.shape
    count = lax.axis_size("trk")
    t = lax.axis_index("trk").astype(jnp.int32)[None]
    whole = channels * count
    n_tracks = head_weight.shape[1]
    group = sequences // 2
    rows = group * length
    cut = (group // 2) * length
    bf16, f32 = jnp.bfloat16, jnp.float32

    edge_shape = jax.ShapeDtypeStruct((SIDE, channels), bf16)
    first, tails, heads = pl.pallas_call(
        functools.partial(first_kernel, group),
        out_shape=(jax.ShapeDtypeStruct((rows, channels), bf16), edge_shape, edge_shape),
        grid=(1,),
        in_specs=[pl.BlockSpec((group, length, channels), lambda i: (0, 0, 0)), ANY, VMEM, VMEM],
        out_specs=(VMEM,) * 3,
        scratch_shapes=[pltpu.VMEM((sequences, 2, EDGE, channels), bf16), pltpu.SemaphoreType.DMA((sequences, 2))],
        compiler_params=pltpu.CompilerParams(vmem_limit_bytes=LIMIT),
        cost_estimate=cost(rows * channels * 20, rows * channels * 6, rows * channels),
    )(activations, activations, norm_gain, norm_bias)
    before, after = passed_along(tails, "pos", 1), passed_along(heads, "pos", -1)
    second = pl.pallas_call(
        second_kernel,
        out_shape=jax.ShapeDtypeStruct((rows + EDGE, channels), bf16),
        grid=(1,),
        in_specs=[pl.BlockSpec((group, length, channels), lambda i: (1, 0, 0))] + [VMEM] * 4,
        out_specs=VMEM,
        compiler_params=pltpu.CompilerParams(vmem_limit_bytes=LIMIT),
        cost_estimate=cost(rows * channels * 20, rows * channels * 6, rows * channels),
    )(activations, norm_gain, norm_bias, before, after)
    first_places, _ = spread(first, cut, rows)
    second_places, wholes = spread(second, cut, rows)
    edges = {j: (array, rows) for j, array in wholes.items()}
    for j in range(1, count):
        low, high = split_bits(j)
        if low != high:
            array, start = edges[j ^ high]
            edges[j] = (swap(array[start : start + EDGE], high), 0)

    def conv(i, places):
        arrays, plan, index = arrays_of(places)
        edge_plan = [(index(edges[j][0]), edges[j][1]) for j in range(count)]
        return pl.pallas_call(
            functools.partial(conv_kernel, i * group, group, plan, edge_plan, len(arrays)),
            out_shape=jax.ShapeDtypeStruct((rows, channels), bf16),
            grid=(1,),
            in_specs=[SMEM, pl.BlockSpec((group, length, channels), lambda _: (i, 0, 0))]
            + [VMEM] * (1 + len(arrays)),
            out_specs=VMEM,
            compiler_params=pltpu.CompilerParams(vmem_limit_bytes=LIMIT),
            cost_estimate=cost(6 * rows * whole * channels, 2 * rows * whole + 6 * whole * channels),
        )(t, activations, conv_weight, *arrays)

    mixed = [spread(conv(i, places), cut, rows)[0] for i, places in enumerate((first_places, second_places))]

    stride = straddle_map.shape[0]
    n_strad = -(-stride // 8) * 8
    sums = ()
    tracks = None
    for i in range(2):
        arrays, plan, _ = arrays_of(mixed[i])
        extra = () if i == 0 else (*sums, tracks)
        tracks, *sums = pl.pallas_call(
            functools.partial(head_kernel, i * group, group, length, plan, len(arrays), i == 1),
            out_shape=(
                jax.ShapeDtypeStruct((sequences, length, n_tracks), bf16),
                jax.ShapeDtypeStruct((GENES_DEV, n_tracks), f32),
                jax.ShapeDtypeStruct((n_strad, n_tracks), f32),
            ),
            in_specs=[SMEM, VMEM, VMEM, VMEM] + [VMEM] * len(arrays) + ([VMEM, VMEM, ANY] if i else []),
            out_specs=(ANY, VMEM, VMEM),
            input_output_aliases={4 + len(arrays) + 2: 0} if i else {},
            scratch_shapes=[
                pltpu.VMEM((group, length, n_tracks), bf16),
                pltpu.SemaphoreType.DMA((group,)),
            ],
            compiler_params=pltpu.CompilerParams(vmem_limit_bytes=LIMIT),
            cost_estimate=cost(
                2 * rows * whole * n_tracks,
                2 * rows * (whole + n_tracks) + 2 * whole * n_tracks,
                2 * rows * n_tracks,
            ),
        )(t, head_weight, head_bias, gene_slot, *arrays, *extra)
    return tracks, gene_mean_of(*sums, gene_slot, straddle_map)


def by_ops(
    activations, norm_gain, norm_bias, conv_weight, head_weight, head_bias, gene_slot, straddle_map
):
    sequences, length, channels = activations.shape
    rows = sequences * length
    f32, bf16 = jnp.float32, jnp.bfloat16
    hidden = gelu_of(activations, norm_gain, norm_bias).astype(bf16)
    gathered = lax.all_gather(hidden, "trk", axis=2, tiled=True)
    padded = jnp.concatenate(
        [passed_along(gathered[:, -1:], "pos", 1), gathered, passed_along(gathered[:, :1], "pos", -1)], axis=1
    )
    total = jnp.zeros((rows, conv_weight.shape[2]), f32)
    for k in range(3):
        window = padded[:, k : k + length].reshape(rows, -1)
        total = total + jnp.dot(window, conv_weight[k], preferred_element_type=f32)
    mixed = (activations.reshape(rows, channels).astype(f32) + total).astype(bf16)
    mixed = lax.all_gather(mixed, "trk", axis=1, tiled=True)
    logits = jnp.dot(mixed, head_weight, preferred_element_type=f32)
    tracks = jax.nn.softplus(logits + head_bias).astype(bf16)
    slots = jnp.arange(GENES_DEV + straddle_map.shape[0], dtype=jnp.int32)
    onehot = (gene_slot.reshape(-1)[None, :] == slots[:, None]).astype(bf16)
    sums = jnp.dot(onehot, tracks, preferred_element_type=f32)
    mean = gene_mean_of(sums[:GENES_DEV], sums[GENES_DEV:], gene_slot, straddle_map)
    return tracks.reshape(sequences, length, -1), mean


def gene_mean_of(own, strad, gene_slot, straddle_map):
    stride = straddle_map.shape[0]
    f32 = jnp.float32
    slots = jnp.arange(GENES_DEV + stride, dtype=jnp.int32)
    counts = jnp.sum((gene_slot.reshape(-1)[None, :] == slots[:, None]).astype(f32), axis=1)
    received_counts = passed_along(counts[GENES_DEV:], "pos", -1)
    owners = (straddle_map[None, :] == jnp.arange(GENES_DEV, dtype=jnp.int32)[:, None]).astype(f32)
    gene_counts = counts[:GENES_DEV] + jnp.sum(owners * received_counts[None], axis=1)
    received = passed_along(strad, "pos", -1)[:stride]
    totals = own + jnp.dot(owners, received, precision=lax.Precision.HIGHEST)
    return totals / jnp.maximum(gene_counts, 1.0)[:, None]


def per_device(*args):
    lanes = args[0].shape[2] % LANES == 0 and args[4].shape[1] % LANES == 0
    return (by_kernels if lanes else by_ops)(*args)


def solution(mesh):
    in_specs = (
        P(None, "pos", "trk"),
        P("trk"),
        P("trk"),
        P(None, None, "trk"),
        P(None, "trk"),
        P("trk"),
        P(None, "pos"),
        P("pos"),
    )
    out_specs = (P(None, "pos", "trk"), P("pos", "trk"))
    return jax.shard_map(
        per_device, mesh=mesh, in_specs=in_specs, out_specs=out_specs, check_vma=False
    )
```

```python
import functools

import jax
import jax.numpy as jnp
from jax import lax
from jax.experimental import pallas as pl
from jax.experimental.pallas import tpu as pltpu
from jax.sharding import PartitionSpec as P


GENES_DEV = 32
LANES = 128
LIMIT = 16 << 20
EDGE = 16
SIDE = 8
VMEM = pl.BlockSpec(memory_space=pltpu.VMEM)
ANY = pl.BlockSpec(memory_space=pl.ANY)
HBM = pl.BlockSpec(memory_space=pltpu.HBM)
SMEM = pl.BlockSpec(memory_space=pltpu.SMEM)


def swap(value, bit):
    count = lax.axis_size("trk")
    return lax.ppermute(value, "trk", [(i, i ^ bit) for i in range(count)])


def swap_pos(value, bit):
    count = lax.axis_size("pos")
    return lax.ppermute(value, "pos", [(i, i ^ bit) for i in range(count)])


def split_bits(j):
    return j & -j, 1 << (j.bit_length() - 1)


def passed_along(value, axis, steps):
    count = lax.axis_size(axis)
    initial, last = (max(0, -steps), min(count, count - steps))
    return lax.ppermute(value, axis, [(source, source + steps) for source in range(initial, last)])


def gelu_of(values, gain, bias):
    return jax.nn.gelu(values.astype(jnp.float32) * gain + bias, approximate=True)


def params(**more):
    return pltpu.CompilerParams(vmem_limit_bytes=LIMIT, **more)


def cost(flops, nbytes, calls=0):
    return pl.CostEstimate(flops=int(flops), bytes_accessed=int(nbytes), transcendentals=int(calls))


def first_kernel(act_ref, gain_ref, bias_ref, *refs):
    sequences, length, channels = act_ref.shape
    outs = refs[:sequences]
    scale_ref, tail_ref, head_ref, edges, gain, bias, sems, edge_sems, scale_sems = refs[sequences:]
    copies = [
        pltpu.make_async_copy(act_ref.at[s], out.at[pl.ds(0, length)], sems.at[s]) for s, out in enumerate(outs)
    ]
    for s in range(sequences):
        for side, start in enumerate((length - EDGE, 0)):
            copies.append(
                pltpu.make_async_copy(act_ref.at[s, pl.ds(start, EDGE)], edges.at[s, side], edge_sems.at[s, side])
            )
    copies.append(pltpu.make_async_copy(gain_ref, gain, scale_sems.at[0]))
    copies.append(pltpu.make_async_copy(bias_ref, bias, scale_sems.at[1]))
    for copy in copies:
        copy.start()
    for copy in copies:
        copy.wait()
    index = lax.broadcasted_iota(jnp.int32, (SIDE, channels), 0)
    scale_ref[...] = jnp.where(index == 0, gain[...][None], bias[...][None])
    tails = jnp.zeros((SIDE, channels), jnp.float32)
    heads = tails
    for s in range(sequences):
        tails = jnp.where(index == s, edges[s, 0].astype(jnp.float32)[EDGE - 1 :], tails)
        heads = jnp.where(index == s, edges[s, 1].astype(jnp.float32)[:1], heads)
    tail_ref[...] = tails.astype(jnp.bfloat16)
    head_ref[...] = heads.astype(jnp.bfloat16)


def second_kernel(block_ref, before_ref, after_ref, out_ref, edges, sem):
    del block_ref
    edges[...] = jnp.concatenate(
        [before_ref[...].astype(jnp.float32), after_ref[...].astype(jnp.float32)]
    ).astype(jnp.bfloat16)
    copy = pltpu.make_async_copy(edges, out_ref.at[pl.ds(out_ref.shape[0] - EDGE, EDGE)], sem)
    copy.start()
    copy.wait()


def join_kernel(n_pieces, count, where_ref, *refs):
    pieces, out_ref, sems = refs[:n_pieces], refs[n_pieces], refs[n_pieces + 1]
    t, pos = where_ref[0], where_ref[1]
    taps, rows, channels = pieces[0].shape
    split = n_pieces // count
    copies = []
    for i, piece in enumerate(pieces):
        place = pos ^ i
        block = (place // split) ^ t
        start = pl.multiple_of((block * split + place % split) * rows, rows)
        for k in range(taps):
            copies.append(
                pltpu.make_async_copy(
                    piece.at[k],
                    out_ref.at[pl.ds(start, rows), pl.ds(k * channels, channels)],
                    sems.at[i, k],
                )
            )
            copies[-1].start()
    for copy in copies:
        copy.wait()


def stage_kernel(count, t_ref, w_ref, head_ref, w_out, head_out, sems):
    taps, _, channels = w_ref.shape
    copies = []
    for j in range(count):
        start = pl.multiple_of((t_ref[0] ^ j) * channels, channels)
        rows = pl.ds(j * channels, channels)
        for k in range(taps):
            copies.append(
                pltpu.make_async_copy(
                    w_ref.at[k, pl.ds(start, channels)],
                    w_out.at[rows, pl.ds(k * channels, channels)],
                    sems.at[j, k],
                )
            )
        copies.append(
            pltpu.make_async_copy(head_ref.at[pl.ds(start, channels)], head_out.at[rows], sems.at[j, taps])
        )
    for copy in copies:
        copy.start()
    for copy in copies:
        copy.wait()


def piece_kernel(pos_ref, w_ref, out_ref, sem):
    rows = out_ref.shape[1]
    start = pl.multiple_of(pos_ref[0] * rows, rows)
    copy = pltpu.make_async_copy(w_ref.at[:, pl.ds(start, rows)], out_ref, sem)
    copy.start()
    copy.wait()


def count_kernel(slot_ref, out_ref):
    sequences, length = slot_ref.shape
    index = lax.broadcasted_iota(jnp.int32, (out_ref.shape[0], length), 0)
    total = jnp.zeros((out_ref.shape[0], 1), jnp.float32)
    for s in range(sequences):
        hit = (index == slot_ref[s : s + 1, :]).astype(jnp.float32)
        total = total + jnp.sum(hit, axis=1, keepdims=True)
    out_ref[...] = jnp.broadcast_to(total, out_ref.shape)


def mean_kernel(map_ref, own_ref, got_ref, count_ref, got_count_ref, out_ref):
    n_own, width = own_ref.shape
    totals, counts = own_ref[...], count_ref[:n_own, :1]
    row = lax.broadcasted_iota(jnp.int32, (n_own, width), 0)
    short = row[:, :1]
    for s in range(map_ref.shape[0]):
        gene = map_ref[s]
        totals = totals + jnp.where(row == gene, got_ref[s : s + 1, :], 0.0)
        counts = counts + jnp.where(short == gene, got_count_ref[s : s + 1, :1], 0.0)
    out_ref[...] = totals / jnp.maximum(counts, 1.0)


def convolved(first, s, values, edge, weight, own):
    length, channels = own.shape
    made = jnp.dot(jnp.concatenate([values, edge]), weight, preferred_element_type=jnp.float32)
    row = lax.broadcasted_iota(jnp.int32, (length, channels), 0)
    before, at, after = (made[:, k * channels : (k + 1) * channels] for k in range(3))
    place = length + first + s
    left = jnp.where(row == 0, before[place : place + 1], pltpu.roll(before[:length], 1, 0))
    place += SIDE
    right = jnp.where(row == length - 1, after[place : place + 1], pltpu.roll(after[:length], length - 1, 0))
    return (own.astype(jnp.float32) + ((left + at[:length]) + right)).astype(jnp.bfloat16)


def conv_kernel(first, group, count, edge_at, ends_ref, w_ref, *refs):
    scales = refs[:count]
    blocks = [refs[count * (1 + s) : count * (2 + s)] for s in range(group)]
    refs = refs[count * (1 + group) :]
    if edge_at is None:
        edge_in, refs = refs[0], refs[1:]
    hidden_ref, refs = refs[0], refs[1:]
    if edge_at is not None:
        edge_out, refs = refs[0], refs[1:]
    outs = refs
    length = hidden_ref.shape[0] // group
    channels = scales[0].shape[1]
    weight = w_ref[...]
    gains = [(scale[0:1, :], scale[1:2, :]) for scale in scales]
    if edge_at is None:
        edge = edge_in[...]
    else:
        row = lax.broadcasted_iota(jnp.int32, (EDGE, channels), 0)
        alive = jnp.where(row < SIDE, ends_ref[0], ends_ref[1]) > 0
        edge = jnp.concatenate(
            [
                jnp.where(alive, gelu_of(blocks[edge_at][j][length : length + EDGE, :], *gains[j]), 0.0)
                for j in range(count)
            ],
            axis=1,
        ).astype(jnp.bfloat16)
        edge_out[...] = edge
    for s in range(group):
        values = jnp.concatenate(
            [gelu_of(blocks[s][j][:length, :], *gains[j]).astype(jnp.bfloat16) for j in range(count)], axis=1
        )
        hidden_ref[s * length : (s + 1) * length, :] = values
        made = convolved(first, s, values, edge, weight, blocks[s][0][:length, :])
        if len(outs) == 1:
            outs[0][s * length : (s + 1) * length, :] = made
        else:
            outs[s][...] = made


def again_kernel(first, group, w_ref, edge_ref, hidden_ref, *refs):
    own, out_ref = refs[:group], refs[group]
    length = hidden_ref.shape[0] // group
    weight = w_ref[...]
    for s in range(group):
        rows = slice(s * length, (s + 1) * length)
        out_ref[rows, :] = convolved(
            first, s, hidden_ref[rows, :], edge_ref[...], weight, own[s][:length, :]
        )


def head_kernel(first, plan, n_blocks, more, w_ref, bias_ref, slot_ref, *refs):
    blocks = refs[:n_blocks]
    refs = refs[n_blocks:]
    if more:
        own_in, strad_in, _ = refs[:3]
        refs = refs[3:]
    tracks_ref, own_ref, strad_ref, made, out_sems = refs
    length = made.shape[1]
    weight = w_ref[...]
    n_own, n_strad = own_ref.shape[0], strad_ref.shape[0]
    index = lax.broadcasted_iota(jnp.int32, (n_own + n_strad, length), 0)
    if more:
        sums = jnp.concatenate([own_in[...], strad_in[...]])
    else:
        sums = jnp.zeros((n_own + n_strad, w_ref.shape[1]), jnp.float32)
    bias = bias_ref[...][None]
    outs = []
    for s, places in enumerate(plan):
        values = jnp.concatenate([blocks[which][row : row + length, :] for which, row in places], axis=1)
        logits = jnp.dot(values, weight, preferred_element_type=jnp.float32) + bias
        part = jnp.maximum(logits, 0.0) + jnp.log1p(jnp.exp(-jnp.abs(logits)))
        made[s] = part.astype(jnp.bfloat16)
        outs.append(pltpu.make_async_copy(made.at[s], tracks_ref.at[first + s], out_sems.at[s]))
        outs[-1].start()
        onehot = (index == slot_ref[first + s : first + s + 1, :]).astype(jnp.bfloat16)
        sums = sums + jnp.dot(onehot, made[s], preferred_element_type=jnp.float32)
    own_ref[...] = sums[:n_own]
    strad_ref[...] = sums[n_own:]
    for copy in outs:
        copy.wait()


def by_kernels(
    activations, norm_gain, norm_bias, conv_weight, head_weight, head_bias, gene_slot, straddle_map
):
    sequences, length, channels = activations.shape
    count, n_pos = lax.axis_size("trk"), lax.axis_size("pos")
    pos = lax.axis_index("pos").astype(jnp.int32)
    t = lax.axis_index("trk").astype(jnp.int32)
    where = jnp.stack([t, pos])
    ends = jnp.stack([(pos > 0).astype(jnp.int32), (pos < n_pos - 1).astype(jnp.int32)])
    whole = channels * count
    n_tracks = head_weight.shape[1]
    group = sequences // 2
    rows = group * length
    bf16, f32 = jnp.bfloat16, jnp.float32
    Shape = jax.ShapeDtypeStruct
    far = [j for j in range(count) if j & (j - 1)]

    piece = whole // n_pos
    mine = pl.pallas_call(
        piece_kernel,
        out_shape=Shape((3, piece, channels), bf16),
        in_specs=[SMEM, ANY],
        out_specs=VMEM,
        scratch_shapes=[pltpu.SemaphoreType.DMA],
        cost_estimate=cost(0, 12 * piece * channels),
    )(pos[None], conv_weight)
    far_weights = {}
    for j in far:
        pieces = {0: swap(mine, j)}
        bit = 2
        while bit < 2 * n_pos:
            step = bit if bit < n_pos else 1
            for i in sorted(pieces):
                pieces[i ^ step] = swap_pos(pieces[i], step)
            bit *= 2
        far_weights[j] = pl.pallas_call(
            functools.partial(join_kernel, n_pos, count),
            out_shape=Shape((whole, 3 * channels), bf16),
            in_specs=[SMEM] + [ANY] * n_pos,
            out_specs=VMEM,
            scratch_shapes=[pltpu.SemaphoreType.DMA((n_pos, 3))],
            compiler_params=params(),
            cost_estimate=cost(0, 12 * whole * channels),
        )(where, *(pieces[i] for i in range(n_pos)))

    taps, heads = pl.pallas_call(
        functools.partial(stage_kernel, count),
        out_shape=[Shape((whole, 3 * channels), bf16), Shape((whole, n_tracks), bf16)],
        in_specs=[SMEM, ANY, ANY],
        out_specs=[VMEM, VMEM],
        scratch_shapes=[pltpu.SemaphoreType.DMA((count, 4))],
        compiler_params=params(),
        cost_estimate=cost(0, 4 * whole * (3 * channels + n_tracks)),
    )(where, conv_weight, head_weight)

    edged = 1
    *blocks, scale, tails, fronts = pl.pallas_call(
        first_kernel,
        out_shape=[Shape((length + EDGE * (s == edged), channels), bf16) for s in range(sequences)]
        + [Shape((SIDE, channels), f32), Shape((SIDE, channels), bf16), Shape((SIDE, channels), bf16)],
        in_specs=[ANY] * 3,
        out_specs=[VMEM] * (sequences + 3),
        scratch_shapes=[
            pltpu.VMEM((sequences, 2, EDGE, channels), bf16),
            pltpu.VMEM((channels,), f32),
            pltpu.VMEM((channels,), f32),
            pltpu.SemaphoreType.DMA((sequences,)),
            pltpu.SemaphoreType.DMA((sequences, 2)),
            pltpu.SemaphoreType.DMA((2,)),
        ],
        cost_estimate=cost(0, 4 * sequences * length * channels),
    )(activations, norm_gain, norm_bias)
    before, after = passed_along(tails, "pos", 1), passed_along(fronts, "pos", -1)
    scales = [scale] + [swap(scale, j) for j in range(1, count)]
    blocks[edged] = pl.pallas_call(
        second_kernel,
        out_shape=Shape((length + EDGE, channels), bf16),
        in_specs=[ANY, VMEM, VMEM],
        out_specs=ANY,
        input_output_aliases={0: 0},
        scratch_shapes=[pltpu.VMEM((EDGE, channels), bf16), pltpu.SemaphoreType.DMA],
        compiler_params=params(),
        cost_estimate=cost(0, 4 * EDGE * channels),
    )(blocks[edged], before, after)
    near = []
    for s in range(sequences):
        found = {0: blocks[s]}
        for j in range(1, count):
            if j not in far:
                found[j] = swap(blocks[s], j)
        for j in far:
            step = split_bits(j)[1 - s % 2]
            found[j] = swap(found[j ^ step], step)
        near.append([found[j] for j in range(count)])

    owned, others = [], []
    edge = None
    for i in range(2):
        seqs = range(i * group, (i + 1) * group)
        edge_at = edged if i == 0 else None
        n_out = 1 if i == 0 else group
        hidden, *made = pl.pallas_call(
            functools.partial(conv_kernel, i * group, group, count, edge_at),
            out_shape=[Shape((rows, whole), bf16)]
            + ([Shape((EDGE, whole), bf16)] if i == 0 else [])
            + [Shape((rows // n_out, channels), bf16)] * n_out,
            in_specs=[SMEM] + [VMEM] * (1 + count * (1 + group) + (i > 0)),
            out_specs=[VMEM] * (1 + (i == 0) + n_out),
            compiler_params=params(),
            cost_estimate=cost(
                6 * rows * whole * channels, 2 * rows * whole + 6 * whole * channels, rows * whole
            ),
        )(ends, taps, *scales, *(block for s in seqs for block in near[s]), *([edge] if i else []))
        if i == 0:
            edge, *made = made
        owned.append(made)
        others.append(
            {
                j: pl.pallas_call(
                    functools.partial(again_kernel, i * group, group),
                    out_shape=Shape((rows, channels), bf16),
                    in_specs=[VMEM] * (3 + group),
                    out_specs=VMEM,
                    compiler_params=params(),
                    cost_estimate=cost(6 * rows * whole * channels, 2 * rows * whole + 6 * whole * channels),
                )(far_weights[j], edge, hidden, *(near[s][j] for s in seqs))
                for j in far
            }
        )

    stride = straddle_map.shape[0]
    n_strad = -(-stride // 8) * 8
    counts = pl.pallas_call(
        count_kernel,
        out_shape=Shape((GENES_DEV + n_strad, LANES), f32),
        in_specs=[VMEM],
        out_specs=VMEM,
        compiler_params=params(),
        cost_estimate=cost(sequences * length * GENES_DEV, 4 * sequences * length),
    )(gene_slot)
    got_counts = passed_along(counts[GENES_DEV:], "pos", -1)
    tracks, sums, done = None, (), 0
    for i in range(2):
        for part, own in enumerate(owned[i]):
            n_seqs = own.shape[0] // length
            arrays = [own] + [others[i][j] if j in far else swap(own, j) for j in range(1, count)]
            plan = [
                [(j, s * length + (part * n_seqs * length if j in far else 0)) for j in range(count)]
                for s in range(n_seqs)
            ]
            tracks, *sums = pl.pallas_call(
                functools.partial(head_kernel, done, plan, count, done > 0),
                out_shape=(
                    Shape((sequences, length, n_tracks), bf16),
                    Shape((GENES_DEV, n_tracks), f32),
                    Shape((n_strad, n_tracks), f32),
                ),
                in_specs=[VMEM] * (3 + count) + ([VMEM, VMEM, ANY] if done else []),
                out_specs=(ANY, VMEM, VMEM),
                input_output_aliases={5 + count: 0} if done else {},
                scratch_shapes=[
                    pltpu.VMEM((n_seqs, length, n_tracks), bf16),
                    pltpu.SemaphoreType.DMA((n_seqs,)),
                ],
                compiler_params=params(),
                cost_estimate=cost(
                    2 * n_seqs * length * whole * n_tracks,
                    2 * n_seqs * length * (whole + n_tracks) + 2 * whole * n_tracks,
                    2 * n_seqs * length * n_tracks,
                ),
            )(heads, head_bias, gene_slot, *arrays, *((*sums, tracks) if done else ()))
            done += n_seqs
    own, strad = sums
    gene_mean = pl.pallas_call(
        mean_kernel,
        out_shape=Shape((GENES_DEV, n_tracks), f32),
        in_specs=[SMEM] + [VMEM] * 4,
        out_specs=VMEM,
        compiler_params=params(),
        cost_estimate=cost(GENES_DEV * n_tracks, 12 * GENES_DEV * n_tracks),
    )(straddle_map, own, passed_along(strad, "pos", -1), counts, got_counts)
    return tracks, gene_mean


def by_ops(
    activations, norm_gain, norm_bias, conv_weight, head_weight, head_bias, gene_slot, straddle_map
):
    sequences, length, channels = activations.shape
    rows = sequences * length
    f32, bf16 = jnp.float32, jnp.bfloat16
    hidden = gelu_of(activations, norm_gain, norm_bias).astype(bf16)
    gathered = lax.all_gather(hidden, "trk", axis=2, tiled=True)
    padded = jnp.concatenate(
        [passed_along(gathered[:, -1:], "pos", 1), gathered, passed_along(gathered[:, :1], "pos", -1)], axis=1
    )
    total = jnp.zeros((rows, conv_weight.shape[2]), f32)
    for k in range(3):
        window = padded[:, k : k + length].reshape(rows, -1)
        total = total + jnp.dot(window, conv_weight[k], preferred_element_type=f32)
    mixed = (activations.reshape(rows, channels).astype(f32) + total).astype(bf16)
    mixed = lax.all_gather(mixed, "trk", axis=1, tiled=True)
    logits = jnp.dot(mixed, head_weight, preferred_element_type=f32)
    tracks = jax.nn.softplus(logits + head_bias).astype(bf16)
    slots = jnp.arange(GENES_DEV + straddle_map.shape[0], dtype=jnp.int32)
    onehot = (gene_slot.reshape(-1)[None, :] == slots[:, None]).astype(bf16)
    sums = jnp.dot(onehot, tracks, preferred_element_type=f32)
    mean = gene_mean_of(sums[:GENES_DEV], sums[GENES_DEV:], gene_slot, straddle_map)
    return tracks.reshape(sequences, length, -1), mean


def gene_mean_of(own, strad, gene_slot, straddle_map):
    stride = straddle_map.shape[0]
    f32 = jnp.float32
    slots = jnp.arange(GENES_DEV + stride, dtype=jnp.int32)
    counts = jnp.sum((gene_slot.reshape(-1)[None, :] == slots[:, None]).astype(f32), axis=1)
    received_counts = passed_along(counts[GENES_DEV:], "pos", -1)
    owners = (straddle_map[None, :] == jnp.arange(GENES_DEV, dtype=jnp.int32)[:, None]).astype(f32)
    gene_counts = counts[:GENES_DEV] + jnp.sum(owners * received_counts[None], axis=1)
    received = passed_along(strad, "pos", -1)[:stride]
    totals = own + jnp.dot(owners, received, precision=lax.Precision.HIGHEST)
    return totals / jnp.maximum(gene_counts, 1.0)[:, None]


def per_device(*args):
    piece = args[3].shape[1] // lax.axis_size("pos")
    lanes = args[0].shape[2] % LANES == 0 and args[4].shape[1] % LANES == 0 and piece % EDGE == 0
    return (by_kernels if lanes else by_ops)(*args)


def solution(mesh):
    in_specs = (
        P(None, "pos", "trk"),
        P("trk"),
        P("trk"),
        P(None, None, "trk"),
        P(None, "trk"),
        P("trk"),
        P(None, "pos"),
        P("pos"),
    )
    out_specs = (P(None, "pos", "trk"), P("pos", "trk"))
    return jax.shard_map(
        per_device, mesh=mesh, in_specs=in_specs, out_specs=out_specs, check_vma=False
    )
```
